512 devices in a mesh: grp: 16 (over y_lo, x, core), mem: 32 (over y_hi, z).
Axes of the slice: x: 4, y: 4 (y_hi: 2, y_lo: 2; y = y_hi * 2 + y_lo), z: 16, core: 2. Of those that a mesh axis runs over, the one named last changes fastest.
Arguments:
- features: float32 [12288, 256], P('mem'), may hold values from -6 to 6
- patterns: bfloat16 [16, 32, 32, 2, 128, 128], P('grp', 'mem'), may hold values from 0 to 2, as said below
- src_tile: int32 [16, 32, 32, 2], P('grp', 'mem'), may hold values from 0 to 2
- dst_tile: int32 [16, 32, 32, 2], P('grp', 'mem'), may hold values from 0 to 2
- tile_count: int32 [16, 32], P('grp', 'mem'), may hold values from 16 to 64, as said below
- cotangent: float32 [12288, 256], P(('mem', 'grp')), may hold values from -6 to 6
- w_self: float32 [256, 256], replicated, may hold values from -0.375 to 0.375
- w_neigh: float32 [256, 256], replicated, may hold values from -0.375 to 0.375
- bias: float32 [256], replicated, may hold values from -3 to 3
Outputs:
- layer_out: float32 [12288, 256], P(('mem', 'grp'))
- grad_self: float32 [256, 256], replicated
- grad_neigh: float32 [256, 256], replicated
- grad_bias: float32 [256], replicated
The draws below stay inside these ranges and needn't reach their ends.
Inputs may be any that keep to these rules, and one draw needn't show every extreme that they name: `tile_count`: some group has all 64 slots live for some destination block. `patterns`: edge weights are zero or positive.
All inputs are finite; a program needn't handle non-finite values.
Results may differ from the reference program's by a relative error of at most 0.0003.
Values sent between devices are 32-bit elements; how exact they have to be, the bound alone decides.
A program may use at most 64 MiB of HBM per device.

```python
import jax
import jax.numpy as jnp
from jax import lax

D_IN = 256
D_OUT = 256
TILE = 128
TBLK = 3
SLOTS = 2
NODES = 12288
N_GRP = 16
N_MEM = 32


def draw_tile_count(key, part):
    first, second = jax.random.split(key)
    most = N_MEM * SLOTS
    base = jax.random.randint(first, (N_GRP * N_MEM,), most // 4, most + 1)
    chosen = jax.random.randint(second, (), 0, N_GRP * N_MEM)
    flat = jnp.where(jnp.arange(N_GRP * N_MEM) == chosen, most, base)
    return flat.reshape(N_GRP, N_MEM).astype(jnp.int32)


def draw_patterns(key, part):
    first, second = jax.random.split(jax.random.fold_in(key, 7))
    shape = (N_GRP, N_MEM, N_MEM, SLOTS, TILE, TILE)
    present = jax.random.uniform(first, shape, jnp.float32) < 0.35
    weights = jax.random.uniform(second, shape, jnp.float32, 0.5, 2.0)
    return jnp.where(present, weights, 0.0).astype(jnp.bfloat16)


def touch_ends(entries, key, smallest, top_value):
    index_at = [jax.random.randint(jax.random.fold_in(key, axis), (), 0, length) for axis, length in enumerate(entries.shape)]
    widest = entries.shape.index(max(entries.shape))
    neighbour = index_at[:widest] + [(index_at[widest] + 1) % entries.shape[widest]] + index_at[widest + 1:]
    return entries.at[tuple(index_at)].set(smallest).at[tuple(neighbour)].set(top_value)


def steps_of(own_key, shape, cuts, smallest, top_value):
    factor_of, own = 1.0, jax.random.fold_in(own_key, 6)
    for dim, shards_of in cuts:
        heights = jnp.exp(jax.random.uniform(jax.random.fold_in(own, dim), (shards_of,), jnp.float32, smallest / len(cuts), top_value / len(cuts)))
        factor_of = factor_of * jnp.repeat(heights, shape[dim] // shards_of).reshape([-1 if axis == dim else 1 for axis in range(len(shape))])
    return factor_of


def bell_draw(own_key, shape, spread, reach, cuts=(), held_as=jnp.bfloat16):
    factor_of = steps_of(own_key, shape, cuts, -0.22, 0.18) if cuts else 1.0
    entries = jax.random.normal(own_key, shape, jnp.float32) * spread * factor_of
    return jnp.minimum(jnp.maximum(entries, -reach), reach).astype(held_as)


def setup_inputs(seed: int = 0) -> dict:
    key_list = jax.random.split(jax.random.key(seed), 10)
    features = bell_draw(key_list[0], (NODES, D_IN), 1.0, 6.0, ((0, 32),), jnp.float32)
    patterns = draw_patterns(jax.random.fold_in(key_list[9], 71), 0)
    src_tile = touch_ends(jax.random.randint(key_list[2], (N_GRP, N_MEM, N_MEM, SLOTS), 0, TBLK), jax.random.fold_in(key_list[2], 1), 0, TBLK - 1).astype(jnp.int32)
    dst_tile = touch_ends(jax.random.randint(key_list[3], (N_GRP, N_MEM, N_MEM, SLOTS), 0, TBLK), jax.random.fold_in(key_list[3], 1), 0, TBLK - 1).astype(jnp.int32)
    tile_count = draw_tile_count(jax.random.fold_in(key_list[9], 71), 0)
    cotangent = bell_draw(key_list[5], (NODES, D_OUT), 1.0, 6.0, ((0, 512),), jnp.float32)
    w_self = bell_draw(key_list[6], (D_IN, D_OUT), D_IN ** -0.5, 0.375, (), jnp.float32)
    w_neigh = bell_draw(key_list[7], (D_IN, D_OUT), D_IN ** -0.5, 0.375, (), jnp.float32)
    bias = bell_draw(key_list[8], (D_OUT,), 0.5, 3.0, (), jnp.float32)
    return {"features": features, "patterns": patterns, "src_tile": src_tile, "dst_tile": dst_tile, "tile_count": tile_count, "cotangent": cotangent, "w_self": w_self, "w_neigh": w_neigh, "bias": bias}


def reference(features, patterns, src_tile, dst_tile, tile_count, cotangent, w_self, w_neigh, bias):
    block = TBLK * TILE
    order = (jnp.arange(N_MEM)[:, None] * SLOTS + jnp.arange(SLOTS)[None, :]).astype(jnp.int32)
    live = (order[None, None] < tile_count[:, :, None, None]).astype(jnp.float32)
    tiles_range = jnp.arange(TBLK).astype(jnp.int32)

    def one_block(target):

        def one_group(dense, group):
            masks = patterns[group, target].astype(jnp.float32)
            place = (dst_tile[group, target][..., None] == tiles_range).astype(jnp.float32) * live[group, target][..., None]
            source = (src_tile[group, target][..., None] == tiles_range).astype(jnp.float32)
            placed = place[:, :, :, None, None] * masks[:, :, None]
            dense = dense + jnp.einsum('jptab,jps->tajsb', placed, source, precision=lax.Precision.HIGHEST).reshape(block, N_MEM * block)
            return (dense, None)
        dense, _ = lax.scan(one_group, jnp.zeros((block, N_MEM * block), jnp.float32), jnp.arange(N_GRP))
        summed = jnp.dot(dense, features, precision=lax.Precision.HIGHEST, preferred_element_type=jnp.float32)
        return (summed, lax.optimization_barrier(jnp.sum(dense, axis=1)))
    summed, degree = lax.map(one_block, jnp.arange(N_MEM))
    summed = summed.reshape(NODES, D_IN)
    degree = degree.reshape(NODES)
    neigh = summed / jnp.sqrt(1.0 + degree)[:, None]
    pre = jnp.dot(features, w_self, precision=lax.Precision.HIGHEST, preferred_element_type=jnp.float32)
    pre = pre + jnp.dot(neigh, w_neigh, precision=lax.Precision.HIGHEST, preferred_element_type=jnp.float32) + bias
    sig = jax.nn.sigmoid(pre)
    layer_out = pre * sig
    dpre = cotangent * sig * (1.0 + pre * (1.0 - sig))
    grad_self = jnp.dot(features.T, dpre, precision=lax.Precision.HIGHEST, preferred_element_type=jnp.float32)
    grad_neigh = jnp.dot(neigh.T, dpre, precision=lax.Precision.HIGHEST, preferred_element_type=jnp.float32)
    grad_bias = lax.optimization_barrier(jnp.sum(dpre, axis=0))
    return (layer_out, grad_self, grad_neigh, grad_bias)
```

```python
import jax
import jax.numpy as jnp
from jax import lax
from jax.experimental import pallas as pl
from jax.experimental.pallas import tpu as pltpu
from jax.sharding import PartitionSpec as P

MESH = pl.DeviceIdType.MESH
HIGH = lax.Precision.HIGHEST
F32 = jnp.float32
NX, NY, NZ = 4, 4, 16
GRP, MEM = 16, 32
TILES = 9


def remote(src, dst, send, recv, dev):
    return pltpu.make_async_remote_copy(
        src_ref=src, dst_ref=dst, send_sem=send, recv_sem=recv, device_id=dev, device_id_type=MESH
    )


def gather_kernel(f_ref, g_ref, zs, zr, ys, yr, ws, wr, xs, xr, cs, cr, own_sem):
    g = lax.axis_index("grp")
    m = lax.axis_index("mem")
    core = g % 2
    x = (g // 2) % NX
    y = (m // NZ) * 2 + g // (2 * NX)
    z = m % NZ
    xp = x % 2

    def dev(x_, y_, z_, c_):
        return ((y_ % 2) * NX + x_) * 2 + c_, (y_ // 2) * NZ + z_

    right_z, left_z = (z + 1) % NZ, (z + NZ - 1) % NZ
    right_y, left_y = (y + 1) % NY, (y + NY - 1) % NY
    right_x, left_x = (x + 1) % NX, (x + NX - 1) % NX
    across_y = (y + 2) % NY

    peers = (
        dev(x, y, right_z, core), dev(x, y, left_z, core),
        dev(x, right_y, z, core), dev(x, left_y, z, core),
        dev(right_x, y, z, core), dev(left_x, y, z, core),
        dev(x, y, z, 1 - core),
    )
    barrier = pltpu.get_barrier_semaphore()
    for peer in peers:
        pl.semaphore_signal(barrier, inc=1, device_id=peer, device_id_type=MESH)
    pl.semaphore_wait(barrier, len(peers))

    def z_of(q):
        t = (q + 1) // 2
        return jnp.where(q % 2 == 1, z + NZ - t, z + t) % NZ

    def piece(q, y_):
        return g_ref.at[z_of(q), core, xp, :, y_]

    own = f_ref.at[core, xp, :, y % 2]
    local = pltpu.make_async_copy(own, piece(0, y), own_sem)
    local.start()
    local.wait()

    def z_copy(q, to, slot):
        return remote(piece(q, y), piece(q, y), zs.at[slot], zr.at[slot], dev(x, y, to, core))

    def near(q, side):
        to = right_y if side == 0 else left_y
        return remote(piece(q, y), piece(q, y), ys.at[q, side], yr.at[q, side], dev(x, to, z, core))

    def far(q, side):
        came, to = (left_y, right_y) if side == 0 else (right_y, left_y)
        part = g_ref.at[z_of(q), core, xp, side, came]
        return remote(part, part, ws.at[q, side], wr.at[q, side], dev(x, to, z, core))

    def cross(q, side):
        to = right_x if side == 0 else left_x
        part = g_ref.at[z_of(q), core, xp, side]
        return remote(part, part, xs.at[q, side], xr.at[q, side], dev(to, y, z, core))

    def swap(q):
        part = g_ref.at[z_of(q), core]
        return remote(part, part, cs.at[q], cr.at[q], dev(x, y, z, 1 - core))

    def step(i, carry):
        @pl.when(i < NZ)
        def _():
            q = i

            @pl.when(q == 0)
            def _():
                z_copy(q, right_z, 1).start()
                z_copy(q, left_z, 2).start()

            @pl.when(q > 0)
            def _():
                z_copy(q, right_z, q).wait_recv()

                @pl.when(q + 2 < NZ)
                def _():
                    z_copy(q, jnp.where(q % 2 == 1, right_z, left_z), q + 2).start()

            near(q, 0).start()
            near(q, 1).start()

        @pl.when((i >= 1) & (i < NZ + 1))
        def _():
            q = i - 1
            near(q, 0).wait_recv()
            far(q, 0).start()
            near(q, 1).wait_recv()
            far(q, 1).start()

        @pl.when((i >= 2) & (i < NZ + 2))
        def _():
            q = i - 2
            far(q, 0).wait_recv()
            cross(q, 0).start()
            far(q, 1).wait_recv()
            cross(q, 1).start()

        @pl.when((i >= 3) & (i < NZ + 3))
        def _():
            q = i - 3
            cross(q, 0).wait_recv()
            cross(q, 1).wait_recv()
            swap(q).start()

        return carry

    lax.fori_loop(0, NZ + 3, step, 0)

    def drain(q, carry):
        @pl.when(q > 0)
        def _():
            z_copy(q, right_z, q).wait_send()

        for side in range(2):
            near(q, side).wait_send()
            far(q, side).wait_send()
            cross(q, side).wait_send()
        swap(q).wait_send()
        swap(q).wait_recv()
        return carry

    lax.fori_loop(0, NZ, drain, 0)


def gather_all(features):
    block, width = features.shape
    rows = block // 16
    view = features.reshape(2, 2, 2, 2, rows, width)
    dma = pltpu.SemaphoreType.DMA
    return pl.pallas_call(
        gather_kernel,
        out_shape=jax.ShapeDtypeStruct((NZ, 2, 2, 2, NY, rows, width), F32),
        in_specs=[pl.BlockSpec(memory_space=pltpu.VMEM)],
        out_specs=pl.BlockSpec(memory_space=pl.ANY),
        scratch_shapes=[
            dma((NZ,)), dma((NZ,)),
            dma((NZ, 2)), dma((NZ, 2)),
            dma((NZ, 2)), dma((NZ, 2)),
            dma((NZ, 2)), dma((NZ, 2)),
            dma((NZ,)), dma((NZ,)),
            dma(()),
        ],
        compiler_params=pltpu.CompilerParams(collective_id=0, has_side_effects=True),
    )(view)


def spread_kernel(src_ref, dst_ref, cnt_ref, w_ref, f_ref, out_ref, hi_ref, lo_ref):
    z = pl.program_id(0)

    @pl.when(z == 0)
    def _():
        out_ref[...] = jnp.zeros_like(out_ref)

    tile = w_ref.shape[-1]
    width = f_ref.shape[-1]
    block = hi_ref.shape[1]
    slots = w_ref.shape[2]
    for yhi in range(2):
        full = f_ref[0, :, yhi].reshape(block, width)
        hi = full.astype(jnp.bfloat16)
        hi_ref[yhi] = hi
        lo_ref[yhi] = (full - hi.astype(F32)).astype(jnp.bfloat16)
    for yhi in range(2):
        for p in range(slots):
            order = (yhi * NZ + z) * slots + p

            @pl.when(order < cnt_ref[0])
            def _():
                take = pl.ds(pl.multiple_of(src_ref[order] * tile, tile), tile)
                give = pl.ds(pl.multiple_of(dst_ref[order] * tile, tile), tile)
                mask = w_ref[yhi, 0, p]
                part = jnp.dot(mask, hi_ref[yhi, take, :], preferred_element_type=F32)
                part += jnp.dot(mask, lo_ref[yhi, take, :], preferred_element_type=F32)
                out_ref[give, :width] += part
                out_ref[give, width:] += mask.astype(F32)


def spread(weights, gathered, sources, targets, count):
    members, slots, tile, _ = weights.shape
    rows, width = gathered.shape[-2:]
    block = 16 * rows
    view = gathered.reshape(NZ, 8, 2, 2 * rows, width)
    return pl.pallas_call(
        spread_kernel,
        out_shape=jax.ShapeDtypeStruct((block, width + tile), F32),
        grid_spec=pltpu.PrefetchScalarGridSpec(
            num_scalar_prefetch=3,
            grid=(NZ,),
            in_specs=[
                pl.BlockSpec((2, 1, slots, tile, tile), lambda z, *_: (0, z, 0, 0, 0)),
                pl.BlockSpec((1, 8, 2, 2 * rows, width), lambda z, *_: (z, 0, 0, 0, 0)),
            ],
            out_specs=pl.BlockSpec((block, width + tile), lambda z, *_: (0, 0)),
            scratch_shapes=[
                pltpu.VMEM((2, block, width), jnp.bfloat16),
                pltpu.VMEM((2, block, width), jnp.bfloat16),
            ],
        ),
        compiler_params=pltpu.CompilerParams(dimension_semantics=("arbitrary",)),
    )(
        sources.reshape(members * slots),
        targets.reshape(members * slots),
        count.reshape(1),
        weights.reshape(2, NZ, slots, tile, tile),
        view,
    )


def owner_of(k):
    return (k % 2) * NZ + (k // 2) * 3


def tail_kernel(
    u_ref, f_ref, cot_ref, ws_ref, wn_ref, b_ref,
    layer_ref, grad_ref, bias_ref,
    r1, part, r2, mine, r3, total, fin,
    s1, q1, s2, q2, s3, q3, s4, q4, s5, q5,
):
    g = lax.axis_index("grp")
    m = lax.axis_index("mem")
    width = f_ref.shape[-1]

    barrier = pltpu.get_barrier_semaphore()

    def greet_grp(k, carry):
        pl.semaphore_signal(barrier, inc=1, device_id=((g + k) % GRP, m), device_id_type=MESH)
        return carry

    def greet_mem(k, carry):
        pl.semaphore_signal(barrier, inc=1, device_id=(g, (m + k) % MEM), device_id_type=MESH)
        return carry

    lax.fori_loop(1, GRP, greet_grp, 0)
    lax.fori_loop(1, MEM, greet_mem, 0)
    pl.semaphore_wait(barrier, GRP + MEM - 2)

    def over_grp(make):
        def begin(k, carry):
            make(k).start()
            return carry

        lax.fori_loop(1, GRP, begin, 0)

    def end_grp(make):
        def end(k, carry):
            make(k).wait()
            return carry

        lax.fori_loop(1, GRP, end, 0)

    def send_sum(k):
        peer = (g + k) % GRP
        return remote(u_ref.at[peer], r1.at[k], s1.at[k], q1.at[k], (peer, m))

    over_grp(send_sum)
    own = f_ref[g]
    pre = jnp.dot(own, ws_ref[...], precision=HIGH, preferred_element_type=F32) + b_ref[...]
    end_grp(send_sum)
    whole = u_ref[g]
    for k in range(1, GRP):
        whole = whole + r1[k]
    degree = jnp.sum(whole[:, width:], axis=1, keepdims=True)
    neigh = whole[:, :width] / jnp.sqrt(1.0 + degree)
    pre = pre + jnp.dot(neigh, wn_ref[...], precision=HIGH, preferred_element_type=F32)
    sig = jax.nn.sigmoid(pre)
    layer_ref[...] = pre * sig
    dpre = cot_ref[...] * sig * (1.0 + pre * (1.0 - sig))
    dims = (((0,), (0,)), ((), ()))
    halves = (own, neigh)
    for n in range(2):
        grad = lax.dot_general(halves[n], dpre, dims, precision=HIGH, preferred_element_type=F32)
        for k in range(8):
            for t in range(8):
                low, col = k * 32 + (t // 2) * 8, (t % 2) * 128
                part[n * 8 + k, t] = grad[low : low + 8, col : col + 128]
    sums = jnp.sum(dpre, axis=0, keepdims=True)
    line = lax.broadcasted_iota(jnp.int32, (8, 128), 0)
    first = jnp.broadcast_to(sums[:, :128], (8, 128))
    second = jnp.broadcast_to(sums[:, 128:], (8, 128))
    bias_tile = jnp.where(line == 0, first, jnp.where(line == 1, second, 0.0))
    for k in range(GRP):
        part[k, 8] = bias_tile

    def send_part(k):
        peer = (g + k) % GRP
        return remote(part.at[peer], r2.at[k], s2.at[k], q2.at[k], (peer, m))

    over_grp(send_part)
    end_grp(send_part)
    acc = part[g]
    for k in range(1, GRP):
        acc = acc + r2[k]
    mine[...] = acc

    def send_tile(k):
        to = owner_of(k)
        away = (to - m + MEM) % MEM
        return remote(mine.at[k], r3.at[away], s3.at[k], q3.at[away], (g, to))

    def start_tile(k, carry):
        @pl.when(owner_of(k) != m)
        def _():
            send_tile(k).start()

        return carry

    lax.fori_loop(0, TILES, start_tile, 0)
    zz = m % NZ
    mine_k = (zz // 3) * 2 + m // NZ
    is_owner = (zz % 3 == 0) & (mine_k < TILES)

    def hand_out(k):
        return remote(total, fin.at[mine_k], s4.at[k], q4.at[mine_k], (g, (m + k) % MEM))

    @pl.when(is_owner)
    def _():
        def arrive(k, carry):
            remote(mine.at[0], r3.at[k], s3.at[0], q3.at[k], (g, (m + k) % MEM)).wait_recv()
            return carry

        lax.fori_loop(1, MEM, arrive, 0)
        acc = mine[mine_k]
        for k in range(1, MEM):
            acc = acc + r3[k]
        total[...] = acc
        fin[mine_k] = acc

        def give(k, carry):
            hand_out(k).start()
            return carry

        lax.fori_loop(1, MEM, give, 0)

    def take_tile(k, carry):
        @pl.when(owner_of(k) != m)
        def _():
            remote(total, fin.at[k], s4.at[0], q4.at[k], (g, owner_of(k))).wait_recv()
            send_tile(k).wait_send()

        return carry

    lax.fori_loop(0, TILES, take_tile, 0)

    def send_fin(k):
        peer = (g + k) % GRP
        return remote(fin.at[pl.ds(0, 8)], grad_ref.at[g], s5.at[k], q5.at[k], (peer, m))

    def recv_fin(k):
        peer = (g + GRP - k) % GRP
        return remote(fin.at[pl.ds(0, 8)], grad_ref.at[peer], s5.at[k], q5.at[k], (peer, m))

    over_grp(send_fin)
    grad_ref[g] = fin[0:8]
    bias_ref[...] = fin[8]

    def finish(k, carry):
        send_fin(k).wait_send()
        recv_fin(k).wait_recv()
        return carry

    lax.fori_loop(1, GRP, finish, 0)

    @pl.when(is_owner)
    def _():
        def done(k, carry):
            hand_out(k).wait_send()
            return carry

        lax.fori_loop(1, MEM, done, 0)


def tail(parts, features, cotangent, w_self, w_neigh, bias):
    block, width = features.shape
    share = cotangent.shape[0]
    wide = parts.shape[1]
    dma = pltpu.SemaphoreType.DMA
    vmem = pl.BlockSpec(memory_space=pltpu.VMEM)
    layer, grads, bias_tile = pl.pallas_call(
        tail_kernel,
        out_shape=(
            jax.ShapeDtypeStruct((share, width), F32),
            jax.ShapeDtypeStruct((GRP, 8, 8, 128), F32),
            jax.ShapeDtypeStruct((8, 128), F32),
        ),
        in_specs=[vmem] * 6,
        out_specs=(vmem, vmem, vmem),
        scratch_shapes=[
            pltpu.VMEM((GRP, share, wide), F32),
            pltpu.VMEM((GRP, TILES, 8, 128), F32),
            pltpu.VMEM((GRP, TILES, 8, 128), F32),
            pltpu.VMEM((TILES, 8, 128), F32),
            pltpu.VMEM((MEM, 8, 128), F32),
            pltpu.VMEM((8, 128), F32),
            pltpu.VMEM((TILES, 8, 128), F32),
            dma((GRP,)), dma((GRP,)),
            dma((GRP,)), dma((GRP,)),
            dma((TILES,)), dma((MEM,)),
            dma((MEM,)), dma((TILES,)),
            dma((GRP,)), dma((GRP,)),
        ],
        compiler_params=pltpu.CompilerParams(collective_id=1, has_side_effects=True),
    )(
        parts.reshape(GRP, share, wide),
        features.reshape(GRP, share, width),
        cotangent,
        w_self,
        w_neigh,
        bias.reshape(1, width),
    )
    full = grads.reshape(2, 32, 2, 8, 128).transpose(0, 1, 3, 2, 4).reshape(2, 256, 256)
    return layer, full[0], full[1], bias_tile[:2].reshape(width)


def on_device(features, patterns, src_tile, dst_tile, tile_count, cotangent, w_self, w_neigh, bias):
    gathered = gather_all(features)
    parts = spread(patterns[0, 0], gathered, src_tile, dst_tile, tile_count)
    return tail(parts, features, cotangent, w_self, w_neigh, bias)


def solution(mesh):
    placed = (
        P("mem", None),
        P("grp", "mem", None, None, None, None),
        P("grp", "mem", None, None),
        P("grp", "mem", None, None),
        P("grp", "mem"),
        P(("mem", "grp"), None),
        P(),
        P(),
        P(),
    )
    return jax.shard_map(
        on_device,
        mesh=mesh,
        in_specs=placed,
        out_specs=(P(("mem", "grp"), None), P(), P(), P()),
        check_vma=False,
    )
```

```python
import jax
import jax.numpy as jnp
from jax import lax
from jax.experimental import pallas as pl
from jax.experimental.pallas import tpu as pltpu
from jax.sharding import PartitionSpec as P

MESH = pl.DeviceIdType.MESH
HIGH = lax.Precision.HIGHEST
F32 = jnp.float32
NX, NY, NZ = 4, 4, 16
GRP, MEM = 16, 32
TILES = 9
LAG = 2


def remote(src, dst, send, recv, dev):
    return pltpu.make_async_remote_copy(
        src_ref=src, dst_ref=dst, send_sem=send, recv_sem=recv, device_id=dev, device_id_type=MESH
    )


def owner_of(k):
    return (k % 2) * NZ + (k // 2) * 3


def kernel(
    src_ref, dst_ref, cnt_ref, f_ref, w_ref, cot_ref, ws_ref, wn_ref, b_ref,
    layer_ref, grad_ref, bias_ref,
    g_ref, pair_ref, acc_ref, deg_ref, u_ref, r1, part, r2, mine, r3, total, fin,
    zs, zr, ys, yr, fs, fr, xs, xr, cs, cr, own_sem,
    s1, q1, s2, q2, s3, q3, s4, q4, s5, q5,
):
    g = lax.axis_index("grp")
    m = lax.axis_index("mem")
    core = g % 2
    x = (g // 2) % NX
    y = (m // NZ) * 2 + g // (2 * NX)
    z = m % NZ
    xp = x % 2
    share, width = f_ref.shape[-2:]
    block = GRP * share
    slots, tile = w_ref.shape[2], w_ref.shape[3]
    tblocks = block // tile

    def dev(x_, y_, z_, c_):
        return ((y_ % 2) * NX + x_) * 2 + c_, (y_ // 2) * NZ + z_

    right_z, left_z = (z + 1) % NZ, (z + NZ - 1) % NZ
    right_y, left_y = (y + 1) % NY, (y + NY - 1) % NY
    right_x, left_x = (x + 1) % NX, (x + NX - 1) % NX

    barrier = pltpu.get_barrier_semaphore()

    def greet_grp(k, carry):
        pl.semaphore_signal(barrier, inc=1, device_id=((g + k) % GRP, m), device_id_type=MESH)
        return carry

    def greet_mem(k, carry):
        pl.semaphore_signal(barrier, inc=1, device_id=(g, (m + k) % MEM), device_id_type=MESH)
        return carry

    for peer in (dev(x, right_y, z, core), dev(x, left_y, z, core)):
        pl.semaphore_signal(barrier, inc=1, device_id=peer, device_id_type=MESH)
    lax.fori_loop(1, GRP, greet_grp, 0)
    lax.fori_loop(1, MEM, greet_mem, 0)
    pl.semaphore_wait(barrier, GRP + MEM)

    def z_of(q):
        t = (q + 1) // 2
        return jnp.where(q % 2 == 1, z + NZ - t, z + t) % NZ

    def piece(q, y_):
        return g_ref.at[z_of(q), core, xp, :, y_]

    own_part = f_ref.at[core, xp, :, y % 2]
    local = pltpu.make_async_copy(own_part, piece(0, y), own_sem)
    local.start()
    acc_ref[...] = jnp.zeros_like(acc_ref)
    deg_ref[...] = jnp.zeros_like(deg_ref)
    local.wait()

    def z_copy(q, to, slot):
        return remote(piece(q, y), piece(q, y), zs.at[slot], zr.at[slot], dev(x, y, to, core))

    def near(q, side):
        to = right_y if side == 0 else left_y
        return remote(piece(q, y), piece(q, y), ys.at[q, side], yr.at[q, side], dev(x, to, z, core))

    def far(q, side):
        came, to = (left_y, right_y) if side == 0 else (right_y, left_y)
        half = g_ref.at[z_of(q), core, xp, side, came]
        return remote(half, half, fs.at[q, side], fr.at[q, side], dev(x, to, z, core))

    def cross(q, side):
        to = right_x if side == 0 else left_x
        half = g_ref.at[z_of(q), core, xp, side]
        return remote(half, half, xs.at[q, side], xr.at[q, side], dev(to, y, z, core))

    def swap(q):
        half = g_ref.at[z_of(q), core]
        return remote(half, half, cs.at[q], cr.at[q], dev(x, y, z, 1 - core))

    def multiply(q):
        zq = z_of(q)
        add = None
        deg = None
        for yhi in range(2):
            rows = g_ref[zq, :, :, :, yhi * 2 : yhi * 2 + 2].reshape(block, width)
            hi = rows.astype(jnp.bfloat16)
            lo = (rows - hi.astype(F32)).astype(jnp.bfloat16)
            for s in range(tblocks):
                pair_ref[yhi, s, :tile] = hi[s * tile : (s + 1) * tile]
                pair_ref[yhi, s, tile:] = lo[s * tile : (s + 1) * tile]
        for yhi in range(2):
            j = yhi * NZ + zq
            for p in range(slots):
                live = j * slots + p < cnt_ref[0, 0]
                mask = w_ref[yhi, zq, p].astype(F32)
                placed = jnp.concatenate(
                    [
                        mask * jnp.where(live & (dst_ref[p, j] == t), 1.0, 0.0)
                        for t in range(tblocks)
                    ],
                    axis=0,
                )
                lhs = placed.astype(jnp.bfloat16)
                both = jnp.concatenate([lhs, lhs], axis=1)
                prod = jnp.dot(both, pair_ref[yhi, src_ref[p, j]], preferred_element_type=F32)
                add = prod if add is None else add + prod
                deg = placed if deg is None else deg + placed
        acc_ref[...] += add
        deg_ref[...] += deg

    def within(i, late):
        return (i >= late) & (i < NZ + late)

    def step(i, carry):
        @pl.when(i < NZ)
        def _():
            q = i

            @pl.when(q == 0)
            def _():
                z_copy(q, right_z, 1).start()
                z_copy(q, left_z, 2).start()

            @pl.when(q > 0)
            def _():
                z_copy(q, right_z, q).wait_recv()

                @pl.when(q + 2 < NZ)
                def _():
                    z_copy(q, jnp.where(q % 2 == 1, right_z, left_z), q + 2).start()

            near(q, 0).start()
            near(q, 1).start()

        @pl.when(within(i, LAG))
        def _():
            q = i - LAG
            near(q, 0).wait_recv()
            far(q, 0).start()
            near(q, 1).wait_recv()
            far(q, 1).start()

        @pl.when(within(i, 2 * LAG))
        def _():
            q = i - 2 * LAG
            far(q, 0).wait_recv()
            cross(q, 0).start()
            far(q, 1).wait_recv()
            cross(q, 1).start()

        @pl.when(within(i, 3 * LAG))
        def _():
            q = i - 3 * LAG
            cross(q, 0).wait_recv()
            cross(q, 1).wait_recv()
            swap(q).start()

        @pl.when(within(i, 4 * LAG))
        def _():
            q = i - 4 * LAG
            swap(q).wait_recv()
            multiply(q)

        return carry

    lax.fori_loop(0, NZ + 4 * LAG, step, 0)

    line = lax.broadcasted_iota(jnp.int32, (8, 128), 0)
    ones = jnp.ones((8, tile), F32)
    lanes = lax.dot_general(
        ones, deg_ref[...], (((1,), (1,)), ((), ())), precision=HIGH, preferred_element_type=F32
    )
    deg_tile = jnp.zeros((8, tile), F32)
    for t in range(tblocks):
        deg_tile = jnp.where(line == t, lanes[:, t * tile : (t + 1) * tile], deg_tile)
    for k in range(GRP):
        u_ref[k, :share] = acc_ref[k * share : (k + 1) * share]
        u_ref[k, share:, :tile] = deg_tile
        u_ref[k, share:, tile:] = deg_tile

    def over_grp(make):
        def begin(k, carry):
            make(k).start()
            return carry

        lax.fori_loop(1, GRP, begin, 0)

    def end_grp(make):
        def end(k, carry):
            make(k).wait()
            return carry

        lax.fori_loop(1, GRP, end, 0)

    def send_sum(k):
        peer = (g + k) % GRP
        return remote(u_ref.at[peer], r1.at[k], s1.at[k], q1.at[k], (peer, m))

    over_grp(send_sum)

    def drain(q, carry):
        @pl.when(q > 0)
        def _():
            z_copy(q, right_z, q).wait_send()

        for side in range(2):
            near(q, side).wait_send()
            far(q, side).wait_send()
            cross(q, side).wait_send()
        swap(q).wait_send()
        return carry

    lax.fori_loop(0, NZ, drain, 0)
    own = f_ref[g // 8, (g // 4) % 2, (g // 2) % 2, g % 2]
    pre = jnp.dot(own, ws_ref[...], precision=HIGH, preferred_element_type=F32) + b_ref[...]
    end_grp(send_sum)
    whole = u_ref[g]
    for k in range(1, GRP):
        whole = whole + r1[k]
    at = g * share + lax.broadcasted_iota(jnp.int32, (share, tile), 0)
    lane = lax.broadcasted_iota(jnp.int32, (share, tile), 1)
    degree = jnp.zeros((share, tile), F32)
    for t in range(tblocks):
        row = jnp.broadcast_to(whole[share + t : share + t + 1, :tile], (share, tile))
        degree = jnp.where(at == t * tile + lane, row, degree)
    degree = jnp.sum(degree, axis=1, keepdims=True)
    neigh = whole[:share] / jnp.sqrt(1.0 + degree)
    pre = pre + jnp.dot(neigh, wn_ref[...], precision=HIGH, preferred_element_type=F32)
    sig = jax.nn.sigmoid(pre)
    layer_ref[...] = pre * sig
    dpre = cot_ref[...] * sig * (1.0 + pre * (1.0 - sig))
    dims = (((0,), (0,)), ((), ()))
    halves = (own, neigh)
    for n in range(2):
        grad = lax.dot_general(halves[n], dpre, dims, precision=HIGH, preferred_element_type=F32)
        for k in range(8):
            for t in range(8):
                low, col = k * 32 + (t // 2) * 8, (t % 2) * 128
                part[n * 8 + k, t] = grad[low : low + 8, col : col + 128]
    sums = jnp.sum(dpre, axis=0, keepdims=True)
    first = jnp.broadcast_to(sums[:, :128], (8, 128))
    second = jnp.broadcast_to(sums[:, 128:], (8, 128))
    bias_tile = jnp.where(line == 0, first, jnp.where(line == 1, second, 0.0))
    for k in range(GRP):
        part[k, 8] = bias_tile

    def send_part(k):
        peer = (g + k) % GRP
        return remote(part.at[peer], r2.at[k], s2.at[k], q2.at[k], (peer, m))

    over_grp(send_part)
    end_grp(send_part)
    acc = part[g]
    for k in range(1, GRP):
        acc = acc + r2[k]
    mine[...] = acc

    def send_tile(k):
        to = owner_of(k)
        away = (to - m + MEM) % MEM
        return remote(mine.at[k], r3.at[away], s3.at[k], q3.at[away], (g, to))

    def start_tile(k, carry):
        @pl.when(owner_of(k) != m)
        def _():
            send_tile(k).start()

        return carry

    lax.fori_loop(0, TILES, start_tile, 0)
    zz = m % NZ
    mine_k = (zz // 3) * 2 + m // NZ
    is_owner = (zz % 3 == 0) & (mine_k < TILES)

    def hand_out(k):
        return remote(total, fin.at[mine_k], s4.at[k], q4.at[mine_k], (g, (m + k) % MEM))

    @pl.when(is_owner)
    def _():
        def arrive(k, carry):
            remote(mine.at[0], r3.at[k], s3.at[0], q3.at[k], (g, (m + k) % MEM)).wait_recv()
            return carry

        lax.fori_loop(1, MEM, arrive, 0)
        acc = mine[mine_k]
        for k in range(1, MEM):
            acc = acc + r3[k]
        total[...] = acc
        fin[mine_k] = acc

        def give(k, carry):
            hand_out(k).start()
            return carry

        lax.fori_loop(1, MEM, give, 0)

    def take_tile(k, carry):
        @pl.when(owner_of(k) != m)
        def _():
            remote(total, fin.at[k], s4.at[0], q4.at[k], (g, owner_of(k))).wait_recv()
            send_tile(k).wait_send()

        return carry

    lax.fori_loop(0, TILES, take_tile, 0)

    def send_fin(k):
        peer = (g + k) % GRP
        return remote(fin.at[pl.ds(0, 8)], grad_ref.at[g], s5.at[k], q5.at[k], (peer, m))

    def recv_fin(k):
        peer = (g + GRP - k) % GRP
        return remote(fin.at[pl.ds(0, 8)], grad_ref.at[peer], s5.at[k], q5.at[k], (peer, m))

    over_grp(send_fin)
    grad_ref[g] = fin[0:8]
    bias_ref[...] = fin[8]

    def finish(k, carry):
        send_fin(k).wait_send()
        recv_fin(k).wait_recv()
        return carry

    lax.fori_loop(1, GRP, finish, 0)

    @pl.when(is_owner)
    def _():
        def done(k, carry):
            hand_out(k).wait_send()
            return carry

        lax.fori_loop(1, MEM, done, 0)


def pack_kernel(layer_ref, tiles_ref, bias_ref, layer_out, self_out, neigh_out, bias_out):
    layer_out[...] = layer_ref[...]
    for n, out in enumerate((self_out, neigh_out)):
        for k in range(8):
            for t in range(8):
                low, col = k * 32 + (t // 2) * 8, (t % 2) * 128
                out[low : low + 8, col : col + 128] = tiles_ref[n * 8 + k, t]
    bias_out[:, :128] = bias_ref[0:1]
    bias_out[:, 128:] = bias_ref[1:2]


def on_device(features, patterns, src_tile, dst_tile, tile_count, cotangent, w_self, w_neigh, bias):
    block, width = features.shape
    share = cotangent.shape[0]
    members, slots, tile, _ = patterns.shape[2:]
    tblocks = block // tile
    dma = pltpu.SemaphoreType.DMA
    vmem = pl.BlockSpec(memory_space=pltpu.VMEM)
    smem = pl.BlockSpec(memory_space=pltpu.SMEM)
    layer, tiles, bias_tile = pl.pallas_call(
        kernel,
        out_shape=(
            jax.ShapeDtypeStruct((share, width), F32),
            jax.ShapeDtypeStruct((GRP, 8, 8, 128), F32),
            jax.ShapeDtypeStruct((8, 128), F32),
        ),
        in_specs=[smem] * 3 + [vmem] * 6,
        out_specs=(vmem, vmem, vmem),
        scratch_shapes=[
            pltpu.VMEM((NZ, 2, 2, 2, NY, share, width), F32),
            pltpu.VMEM((2, tblocks, 2 * tile, width), jnp.bfloat16),
            pltpu.VMEM((block, width), F32),
            pltpu.VMEM((block, tile), F32),
            pltpu.VMEM((GRP, share + 8, width), F32),
            pltpu.VMEM((GRP, share + 8, width), F32),
            pltpu.VMEM((GRP, TILES, 8, 128), F32),
            pltpu.VMEM((GRP, TILES, 8, 128), F32),
            pltpu.VMEM((TILES, 8, 128), F32),
            pltpu.VMEM((MEM, 8, 128), F32),
            pltpu.VMEM((8, 128), F32),
            pltpu.VMEM((TILES, 8, 128), F32),
            dma((NZ,)), dma((NZ,)),
            dma((NZ, 2)), dma((NZ, 2)),
            dma((NZ, 2)), dma((NZ, 2)),
            dma((NZ, 2)), dma((NZ, 2)),
            dma((NZ,)), dma((NZ,)),
            dma(()),
            dma((GRP,)), dma((GRP,)),
            dma((GRP,)), dma((GRP,)),
            dma((TILES,)), dma((MEM,)),
            dma((MEM,)), dma((TILES,)),
            dma((GRP,)), dma((GRP,)),
        ],
        compiler_params=pltpu.CompilerParams(collective_id=0, has_side_effects=True),
    )(
        src_tile[0, 0].T,
        dst_tile[0, 0].T,
        tile_count,
        features.reshape(2, 2, 2, 2, share, width),
        patterns.reshape(2, NZ, slots, tile, tile),
        cotangent,
        w_self,
        w_neigh,
        bias.reshape(1, width),
    )
    layer, grad_self, grad_neigh, grad_bias = pl.pallas_call(
        pack_kernel,
        out_shape=(
            jax.ShapeDtypeStruct((share, width), F32),
            jax.ShapeDtypeStruct((width, width), F32),
            jax.ShapeDtypeStruct((width, width), F32),
            jax.ShapeDtypeStruct((1, width), F32),
        ),
        in_specs=[vmem] * 3,
        out_specs=(vmem,) * 4,
    )(layer, tiles, bias_tile)
    return layer, grad_self, grad_neigh, grad_bias.reshape(width)


def solution(mesh):
    placed = (
        P("mem", None),
        P("grp", "mem", None, None, None, None),
        P("grp", "mem", None, None),
        P("grp", "mem", None, None),
        P("grp", "mem"),
        P(("mem", "grp"), None),
        P(),
        P(),
        P(),
    )
    return jax.shard_map(
        on_device,
        mesh=mesh,
        in_specs=placed,
        out_specs=(P(("mem", "grp"), None), P(), P(), P()),
        check_vma=False,
    )
```

```python
import jax
import jax.numpy as jnp
from jax import lax
from jax.experimental import pallas as pl
from jax.experimental.pallas import tpu as pltpu
from jax.sharding import PartitionSpec as P

MESH = pl.DeviceIdType.MESH
HIGH = lax.Precision.HIGHEST
F32 = jnp.float32
NX, NY, NZ = 4, 4, 16
GRP, MEM = 16, 32
TILES = 9
LAG = 2


def remote(src, dst, send, recv, dev):
    return pltpu.make_async_remote_copy(
        src_ref=src, dst_ref=dst, send_sem=send, recv_sem=recv, device_id=dev, device_id_type=MESH
    )


def owner_of(k):
    return (k % 2) * NZ + (k // 2) * 3


def kernel(
    src_ref, dst_ref, cnt_ref, f_ref, w_ref, rows_ref, cot_ref, ws_ref, wn_ref, b_ref,
    layer_ref, grad_ref, bias_ref,
    g_ref, pair_ref, acc_ref, deg_ref, u_ref, r1, part, r2, mine, r3, total, fin,
    zs, zr, es, er, ys, yr, fs, fr, xs, xr, cs, cr, own_sem,
    s1, q1, s2, q2, s3, q3, s4, q4, s5, q5,
):
    g = lax.axis_index("grp")
    m = lax.axis_index("mem")
    core = g % 2
    x = (g // 2) % NX
    y = (m // NZ) * 2 + g // (2 * NX)
    z = m % NZ
    xp = x % 2
    share, width = rows_ref.shape[-2:]
    block = GRP * share
    slots, tile = w_ref.shape[2], w_ref.shape[3]
    tblocks = block // tile

    def dev(x_, y_, z_, c_):
        return ((y_ % 2) * NX + x_) * 2 + c_, (y_ // 2) * NZ + z_

    right_z, left_z = (z + 1) % NZ, (z + NZ - 1) % NZ
    near_y, far_y = y + 1 - 2 * (y % 2), NY - 1 - y

    def place(y_):
        return jnp.where((y_ == 1) | (y_ == 2), 1 + y_, y_ // 3)

    right_x, left_x = (x + 1) % NX, (x + NX - 1) % NX

    barrier = pltpu.get_barrier_semaphore()

    def greet_grp(k, carry):
        pl.semaphore_signal(barrier, inc=1, device_id=((g + k) % GRP, m), device_id_type=MESH)
        return carry

    for peer in (dev(x, far_y, z, core), dev(x, y, right_z, core), dev(x, y, left_z, core)):
        pl.semaphore_signal(barrier, inc=1, device_id=peer, device_id_type=MESH)
    lax.fori_loop(1, GRP, greet_grp, 0)
    pl.semaphore_wait(barrier, GRP + 2)

    def z_of(q):
        t = (q + 1) // 2
        return jnp.where(q % 2 == 1, z + NZ - t, z + t) % NZ

    def piece(q, y_):
        return g_ref.at[z_of(q), core, pl.ds(xp, 2), :, place(y_)]

    own_part = f_ref.at[core, pl.ds(xp, 2), :, y % 2]
    local = pltpu.make_async_copy(own_part, piece(0, y), own_sem)
    local.start()
    trade = remote(own_part, piece(0, y), es, er, dev(x, far_y, z, core))
    trade.start()
    acc_ref[...] = jnp.zeros_like(acc_ref)
    deg_ref[...] = jnp.zeros_like(deg_ref)
    local.wait()

    def z_copy(q, to, slot, which):
        part_ = piece(q, y if which == 0 else far_y)
        return remote(part_, part_, zs.at[slot, which], zr.at[slot, which], dev(x, y, to, core))

    def near(q):
        return remote(piece(q, y), piece(q, y), ys.at[q], yr.at[q], dev(x, near_y, z, core))

    def far(q):
        came = piece(q, near_y)
        return remote(came, came, fs.at[q], fr.at[q], dev(x, far_y, z, core))

    def cross(q, side):
        to = right_x if side == 0 else left_x
        half = g_ref.at[z_of(q), core, 2 * xp, side]
        return remote(half, half, xs.at[q, side], xr.at[q, side], dev(to, y, z, core))

    def swap(q):
        half = g_ref.at[z_of(q), core]
        return remote(half, half, cs.at[q], cr.at[q], dev(x, y, z, 1 - core))

    def multiply(q):
        zq = z_of(q)
        add = None
        deg = None
        for yhi in range(2):
            low, high = (0, 2) if yhi == 0 else (3, 1)
            rows = jnp.stack(
                [g_ref[zq, :, :, :, low], g_ref[zq, :, :, :, high]], axis=3
            ).reshape(block, width)
            hi = rows.astype(jnp.bfloat16)
            lo = (rows - hi.astype(F32)).astype(jnp.bfloat16)
            for s in range(tblocks):
                pair_ref[yhi, s, :tile] = hi[s * tile : (s + 1) * tile]
                pair_ref[yhi, s, tile:] = lo[s * tile : (s + 1) * tile]
        for yhi in range(2):
            j = yhi * NZ + zq
            for p in range(slots):
                live = j * slots + p < cnt_ref[0, 0]
                mask = w_ref[yhi, zq, p].astype(F32)
                placed = jnp.concatenate(
                    [
                        mask * jnp.where(live & (dst_ref[p, j] == t), 1.0, 0.0)
                        for t in range(tblocks)
                    ],
                    axis=0,
                )
                lhs = placed.astype(jnp.bfloat16)
                both = jnp.concatenate([lhs, lhs], axis=1)
                prod = jnp.dot(both, pair_ref[yhi, src_ref[p, j]], preferred_element_type=F32)
                add = prod if add is None else add + prod
                deg = placed if deg is None else deg + placed
        acc_ref[...] += add
        deg_ref[...] += deg

    def within(i, late):
        return (i >= late) & (i < NZ + late)

    def step(i, carry):
        @pl.when(i < NZ)
        def _():
            q = i

            for which in range(2):
                @pl.when(q == 0)
                def _():
                    if which == 1:
                        trade.wait_recv()
                    z_copy(q, right_z, 1, which).start()
                    z_copy(q, left_z, 2, which).start()

                @pl.when(q > 0)
                def _():
                    z_copy(q, right_z, q, which).wait_recv()

                    @pl.when(q + 2 < NZ)
                    def _():
                        to = jnp.where(q % 2 == 1, right_z, left_z)
                        z_copy(q, to, q + 2, which).start()

                if which == 0:
                    near(q).start()

        @pl.when(within(i, LAG))
        def _():
            q = i - LAG
            near(q).wait_recv()
            far(q).start()

        @pl.when(within(i, 2 * LAG))
        def _():
            q = i - 2 * LAG
            far(q).wait_recv()
            cross(q, 0).start()
            cross(q, 1).start()

        @pl.when(within(i, 3 * LAG))
        def _():
            q = i - 3 * LAG
            cross(q, 0).wait_recv()
            cross(q, 1).wait_recv()
            swap(q).start()

        @pl.when(within(i, 4 * LAG))
        def _():
            q = i - 4 * LAG
            swap(q).wait_recv()
            multiply(q)

        return carry

    lax.fori_loop(0, NZ + 4 * LAG, step, 0)

    line = lax.broadcasted_iota(jnp.int32, (8, 128), 0)
    ones = jnp.ones((8, tile), F32)
    lanes = lax.dot_general(
        ones, deg_ref[...], (((1,), (1,)), ((), ())), precision=HIGH, preferred_element_type=F32
    )
    deg_tile = jnp.zeros((8, tile), F32)
    for t in range(tblocks):
        deg_tile = jnp.where(line == t, lanes[:, t * tile : (t + 1) * tile], deg_tile)
    for k in range(GRP):
        u_ref[k, :share] = acc_ref[k * share : (k + 1) * share]
        u_ref[k, share:, :tile] = deg_tile
        u_ref[k, share:, tile:] = deg_tile

    def over_grp(make):
        def begin(k, carry):
            make(k).start()
            return carry

        lax.fori_loop(1, GRP, begin, 0)

    def end_grp(make):
        def end(k, carry):
            make(k).wait()
            return carry

        lax.fori_loop(1, GRP, end, 0)

    def send_sum(k):
        peer = (g + k) % GRP
        return remote(u_ref.at[peer], r1.at[k], s1.at[k], q1.at[k], (peer, m))

    over_grp(send_sum)

    def drain(q, carry):
        @pl.when(q > 0)
        def _():
            for which in range(2):
                z_copy(q, right_z, q, which).wait_send()

        near(q).wait_send()
        far(q).wait_send()
        for side in range(2):
            cross(q, side).wait_send()
        swap(q).wait_send()
        return carry

    trade.wait_send()
    lax.fori_loop(0, NZ, drain, 0)
    own = rows_ref[g]
    pre = jnp.dot(own, ws_ref[...], precision=HIGH, preferred_element_type=F32) + b_ref[...]
    end_grp(send_sum)
    whole = u_ref[g]
    for k in range(1, GRP):
        whole = whole + r1[k]
    at = g * share + lax.broadcasted_iota(jnp.int32, (share, tile), 0)
    lane = lax.broadcasted_iota(jnp.int32, (share, tile), 1)
    degree = jnp.zeros((share, tile), F32)
    for t in range(tblocks):
        row = jnp.broadcast_to(whole[share + t : share + t + 1, :tile], (share, tile))
        degree = jnp.where(at == t * tile + lane, row, degree)
    degree = jnp.sum(degree, axis=1, keepdims=True)
    neigh = whole[:share] / jnp.sqrt(1.0 + degree)
    pre = pre + jnp.dot(neigh, wn_ref[...], precision=HIGH, preferred_element_type=F32)
    sig = jax.nn.sigmoid(pre)
    layer_ref[...] = pre * sig
    dpre = cot_ref[...] * sig * (1.0 + pre * (1.0 - sig))
    dims = (((0,), (0,)), ((), ()))
    halves = (own, neigh)
    for n in range(2):
        grad = lax.dot_general(halves[n], dpre, dims, precision=HIGH, preferred_element_type=F32)
        for k in range(8):
            for t in range(8):
                low, col = k * 32 + (t // 2) * 8, (t % 2) * 128
                part[n * 8 + k, t] = grad[low : low + 8, col : col + 128]
    sums = jnp.sum(dpre, axis=0, keepdims=True)
    first = jnp.broadcast_to(sums[:, :128], (8, 128))
    second = jnp.broadcast_to(sums[:, 128:], (8, 128))
    bias_tile = jnp.where(line == 0, first, jnp.where(line == 1, second, 0.0))
    for k in range(GRP):
        part[k, 8] = bias_tile

    def send_part(k):
        peer = (g + k) % GRP
        return remote(part.at[peer], r2.at[k], s2.at[k], q2.at[k], (peer, m))

    over_grp(send_part)
    end_grp(send_part)
    acc = part[g]
    for k in range(1, GRP):
        acc = acc + r2[k]
    mine[...] = acc

    def send_tile(k):
        to = owner_of(k)
        away = (to - m + MEM) % MEM
        return remote(mine.at[k], r3.at[away], s3.at[k], q3.at[away], (g, to))

    def start_tile(k, carry):
        @pl.when(owner_of(k) != m)
        def _():
            send_tile(k).start()

        return carry

    lax.fori_loop(0, TILES, start_tile, 0)
    zz = m % NZ
    mine_k = (zz // 3) * 2 + m // NZ
    is_owner = (zz % 3 == 0) & (mine_k < TILES)

    def hand_out(k):
        return remote(total, fin.at[mine_k], s4.at[k], q4.at[mine_k], (g, (m + k) % MEM))

    @pl.when(is_owner)
    def _():
        def arrive(k, carry):
            remote(mine.at[0], r3.at[k], s3.at[0], q3.at[k], (g, (m + k) % MEM)).wait_recv()
            return carry

        lax.fori_loop(1, MEM, arrive, 0)
        acc = mine[mine_k]
        for k in range(1, MEM):
            acc = acc + r3[k]
        total[...] = acc
        fin[mine_k] = acc

        def give(k, carry):
            hand_out(k).start()
            return carry

        lax.fori_loop(1, MEM, give, 0)

    def take_tile(k, carry):
        @pl.when(owner_of(k) != m)
        def _():
            remote(total, fin.at[k], s4.at[0], q4.at[k], (g, owner_of(k))).wait_recv()
            send_tile(k).wait_send()

        return carry

    lax.fori_loop(0, TILES, take_tile, 0)

    def send_fin(k):
        peer = (g + k) % GRP
        return remote(fin.at[pl.ds(0, 8)], grad_ref.at[g], s5.at[k], q5.at[k], (peer, m))

    def recv_fin(k):
        peer = (g + GRP - k) % GRP
        return remote(fin.at[pl.ds(0, 8)], grad_ref.at[peer], s5.at[k], q5.at[k], (peer, m))

    over_grp(send_fin)
    grad_ref[g] = fin[0:8]
    bias_ref[...] = fin[8]

    def finish(k, carry):
        send_fin(k).wait_send()
        recv_fin(k).wait_recv()
        return carry

    lax.fori_loop(1, GRP, finish, 0)

    @pl.when(is_owner)
    def _():
        def done(k, carry):
            hand_out(k).wait_send()
            return carry

        lax.fori_loop(1, MEM, done, 0)


def pack_kernel(layer_ref, tiles_ref, bias_ref, layer_out, self_out, neigh_out, bias_out):
    layer_out[...] = layer_ref[...]
    for n, out in enumerate((self_out, neigh_out)):
        for k in range(8):
            for t in range(8):
                low, col = k * 32 + (t // 2) * 8, (t % 2) * 128
                out[low : low + 8, col : col + 128] = tiles_ref[n * 8 + k, t]
    bias_out[:, :128] = bias_ref[0:1]
    bias_out[:, 128:] = bias_ref[1:2]


def on_device(features, patterns, src_tile, dst_tile, tile_count, cotangent, w_self, w_neigh, bias):
    block, width = features.shape
    share = cotangent.shape[0]
    members, slots, tile, _ = patterns.shape[2:]
    tblocks = block // tile
    dma = pltpu.SemaphoreType.DMA
    vmem = pl.BlockSpec(memory_space=pltpu.VMEM)
    smem = pl.BlockSpec(memory_space=pltpu.SMEM)
    layer, tiles, bias_tile = pl.pallas_call(
        kernel,
        out_shape=(
            jax.ShapeDtypeStruct((share, width), F32),
            jax.ShapeDtypeStruct((GRP, 8, 8, 128), F32),
            jax.ShapeDtypeStruct((8, 128), F32),
        ),
        in_specs=[smem] * 3 + [vmem] * 7,
        out_specs=(vmem, vmem, vmem),
        scratch_shapes=[
            pltpu.VMEM((NZ, 2, 3, 2, NY, block // 24, width), F32),
            pltpu.VMEM((2, tblocks, 2 * tile, width), jnp.bfloat16),
            pltpu.VMEM((block, width), F32),
            pltpu.VMEM((block, tile), F32),
            pltpu.VMEM((GRP, share + 8, width), F32),
            pltpu.VMEM((GRP, share + 8, width), F32),
            pltpu.VMEM((GRP, TILES, 8, 128), F32),
            pltpu.VMEM((GRP, TILES, 8, 128), F32),
            pltpu.VMEM((TILES, 8, 128), F32),
            pltpu.VMEM((MEM, 8, 128), F32),
            pltpu.VMEM((8, 128), F32),
            pltpu.VMEM((TILES, 8, 128), F32),
            dma((NZ, 2)), dma((NZ, 2)),
            dma(()), dma(()),
            dma((NZ,)), dma((NZ,)),
            dma((NZ,)), dma((NZ,)),
            dma((NZ, 2)), dma((NZ, 2)),
            dma((NZ,)), dma((NZ,)),
            dma(()),
            dma((GRP,)), dma((GRP,)),
            dma((GRP,)), dma((GRP,)),
            dma((TILES,)), dma((MEM,)),
            dma((MEM,)), dma((TILES,)),
            dma((GRP,)), dma((GRP,)),
        ],
        compiler_params=pltpu.CompilerParams(collective_id=0, has_side_effects=True),
    )(
        src_tile[0, 0].T,
        dst_tile[0, 0].T,
        tile_count,
        features.reshape(2, 3, 2, 2, block // 24, width),
        patterns.reshape(2, NZ, slots, tile, tile),
        features.reshape(GRP, share, width),
        cotangent,
        w_self,
        w_neigh,
        bias.reshape(1, width),
    )
    layer, grad_self, grad_neigh, grad_bias = pl.pallas_call(
        pack_kernel,
        out_shape=(
            jax.ShapeDtypeStruct((share, width), F32),
            jax.ShapeDtypeStruct((width, width), F32),
            jax.ShapeDtypeStruct((width, width), F32),
            jax.ShapeDtypeStruct((1, width), F32),
        ),
        in_specs=[vmem] * 3,
        out_specs=(vmem,) * 4,
    )(layer, tiles, bias_tile)
    return layer, grad_self, grad_neigh, grad_bias.reshape(width)


def solution(mesh):
    placed = (
        P("mem", None),
        P("grp", "mem", None, None, None, None),
        P("grp", "mem", None, None),
        P("grp", "mem", None, None),
        P("grp", "mem"),
        P(("mem", "grp"), None),
        P(),
        P(),
        P(),
    )
    return jax.shard_map(
        on_device,
        mesh=mesh,
        in_specs=placed,
        out_specs=(P(("mem", "grp"), None), P(), P(), P()),
        check_vma=False,
    )
```

```python
import jax
import jax.numpy as jnp
from jax import lax
from jax.experimental import pallas as pl
from jax.experimental.pallas import tpu as pltpu
from jax.sharding import PartitionSpec as P

MESH = pl.DeviceIdType.MESH
HIGH = lax.Precision.HIGHEST
F32 = jnp.float32
NX, NY, NZ = 4, 4, 16
GRP, MEM = 16, 32
TILES = 9
LAG = 2


def remote(src, dst, send, recv, dev):
    return pltpu.make_async_remote_copy(
        src_ref=src, dst_ref=dst, send_sem=send, recv_sem=recv, device_id=dev, device_id_type=MESH
    )


def owner_of(k):
    return (k % 2) * NZ + (k // 2) * 3


def kernel(
    src_ref, dst_ref, cnt_ref, f_ref, w_ref, cot_ref, ws_ref, wn_ref, b_ref,
    layer_ref, grad_ref, bias_ref,
    g_ref, pair_ref, acc_ref, deg_ref, u_ref, r1, part, r2, mine, r3, total, fin,
    zs, zr, ys, yr, fs, fr, xs, xr, cs, cr, own_sem,
    s1, q1, s2, q2, s3, q3, s4, q4, s5, q5,
):
    g = lax.axis_index("grp")
    m = lax.axis_index("mem")
    core = g % 2
    x = (g // 2) % NX
    y = (m // NZ) * 2 + g // (2 * NX)
    z = m % NZ
    xp = x % 2
    share, width = f_ref.shape[-2:]
    block = GRP * share
    slots, tile = w_ref.shape[2], w_ref.shape[3]
    tblocks = block // tile

    def dev(x_, y_, z_, c_):
        return ((y_ % 2) * NX + x_) * 2 + c_, (y_ // 2) * NZ + z_

    right_z, left_z = (z + 1) % NZ, (z + NZ - 1) % NZ
    right_y, left_y = (y + 1) % NY, (y + NY - 1) % NY
    right_x, left_x = (x + 1) % NX, (x + NX - 1) % NX

    barrier = pltpu.get_barrier_semaphore()

    def greet_grp(k, carry):
        pl.semaphore_signal(barrier, inc=1, device_id=((g + k) % GRP, m), device_id_type=MESH)
        return carry

    for peer in (dev(x, NY - 1 - y, z, core), dev(x, y, right_z, core), dev(x, y, left_z, core)):
        pl.semaphore_signal(barrier, inc=1, device_id=peer, device_id_type=MESH)
    lax.fori_loop(1, GRP, greet_grp, 0)
    pl.semaphore_wait(barrier, GRP + 2)

    def z_of(q):
        t = (q + 1) // 2
        return jnp.where(q % 2 == 1, z + NZ - t, z + t) % NZ

    def piece(q, y_):
        return g_ref.at[z_of(q), core, xp, :, y_]

    own_part = f_ref.at[core, xp, :, y % 2]
    local = pltpu.make_async_copy(own_part, piece(0, y), own_sem)
    local.start()
    acc_ref[...] = jnp.zeros_like(acc_ref)
    deg_ref[...] = jnp.zeros_like(deg_ref)
    local.wait()

    def z_copy(q, to, slot):
        return remote(piece(q, y), piece(q, y), zs.at[slot], zr.at[slot], dev(x, y, to, core))

    def near(q, side):
        to = right_y if side == 0 else left_y
        return remote(piece(q, y), piece(q, y), ys.at[q, side], yr.at[q, side], dev(x, to, z, core))

    def far(q, side):
        came, to = (left_y, right_y) if side == 0 else (right_y, left_y)
        half = g_ref.at[z_of(q), core, xp, side, came]
        return remote(half, half, fs.at[q, side], fr.at[q, side], dev(x, to, z, core))

    def cross(q, side):
        to = right_x if side == 0 else left_x
        half = g_ref.at[z_of(q), core, xp, side]
        return remote(half, half, xs.at[q, side], xr.at[q, side], dev(to, y, z, core))

    def swap(q):
        half = g_ref.at[z_of(q), core]
        return remote(half, half, cs.at[q], cr.at[q], dev(x, y, z, 1 - core))

    def multiply(q):
        zq = z_of(q)
        add = None
        deg = None
        for yhi in range(2):
            rows = g_ref[zq, :, :, :, yhi * 2 : yhi * 2 + 2].reshape(block, width)
            hi = rows.astype(jnp.bfloat16)
            lo = (rows - hi.astype(F32)).astype(jnp.bfloat16)
            for s in range(tblocks):
                pair_ref[yhi, s, :tile] = hi[s * tile : (s + 1) * tile]
                pair_ref[yhi, s, tile:] = lo[s * tile : (s + 1) * tile]
        for yhi in range(2):
            j = yhi * NZ + zq
            for p in range(slots):
                live = j * slots + p < cnt_ref[0, 0]
                mask = w_ref[yhi, zq, p].astype(F32)
                placed = jnp.concatenate(
                    [
                        mask * jnp.where(live & (dst_ref[p, j] == t), 1.0, 0.0)
                        for t in range(tblocks)
                    ],
                    axis=0,
                )
                lhs = placed.astype(jnp.bfloat16)
                both = jnp.concatenate([lhs, lhs], axis=1)
                prod = jnp.dot(both, pair_ref[yhi, src_ref[p, j]], preferred_element_type=F32)
                add = prod if add is None else add + prod
                deg = placed if deg is None else deg + placed
        acc_ref[...] += add
        deg_ref[...] += deg

    def within(i, late):
        return (i >= late) & (i < NZ + late)

    def step(i, carry):
        @pl.when(i < NZ)
        def _():
            q = i

            @pl.when(q == 0)
            def _():
                z_copy(q, right_z, 1).start()
                z_copy(q, left_z, 2).start()

            @pl.when(q > 0)
            def _():
                z_copy(q, right_z, q).wait_recv()

                @pl.when(q + 2 < NZ)
                def _():
                    z_copy(q, jnp.where(q % 2 == 1, right_z, left_z), q + 2).start()

            near(q, 0).start()
            near(q, 1).start()

        @pl.when(within(i, LAG))
        def _():
            q = i - LAG
            near(q, 0).wait_recv()
            far(q, 0).start()
            near(q, 1).wait_recv()
            far(q, 1).start()

        @pl.when(within(i, 2 * LAG))
        def _():
            q = i - 2 * LAG
            far(q, 0).wait_recv()
            cross(q, 0).start()
            far(q, 1).wait_recv()
            cross(q, 1).start()

        @pl.when(within(i, 3 * LAG))
        def _():
            q = i - 3 * LAG
            cross(q, 0).wait_recv()
            cross(q, 1).wait_recv()
            swap(q).start()

        @pl.when(within(i, 4 * LAG))
        def _():
            q = i - 4 * LAG
            swap(q).wait_recv()
            multiply(q)

        return carry

    lax.fori_loop(0, NZ + 4 * LAG, step, 0)

    line = lax.broadcasted_iota(jnp.int32, (8, 128), 0)
    ones = jnp.ones((8, tile), F32)
    lanes = lax.dot_general(
        ones, deg_ref[...], (((1,), (1,)), ((), ())), precision=HIGH, preferred_element_type=F32
    )
    deg_tile = jnp.zeros((8, tile), F32)
    for t in range(tblocks):
        deg_tile = jnp.where(line == t, lanes[:, t * tile : (t + 1) * tile], deg_tile)
    for k in range(GRP):
        u_ref[k, :share] = acc_ref[k * share : (k + 1) * share]
        u_ref[k, share:, :tile] = deg_tile
        u_ref[k, share:, tile:] = deg_tile

    def over_grp(make):
        def begin(k, carry):
            make(k).start()
            return carry

        lax.fori_loop(1, GRP, begin, 0)

    def end_grp(make):
        def end(k, carry):
            make(k).wait()
            return carry

        lax.fori_loop(1, GRP, end, 0)

    def send_sum(k):
        peer = (g + k) % GRP
        return remote(u_ref.at[peer], r1.at[k], s1.at[k], q1.at[k], (peer, m))

    over_grp(send_sum)

    def drain(q, carry):
        @pl.when(q > 0)
        def _():
            z_copy(q, right_z, q).wait_send()

        for side in range(2):
            near(q, side).wait_send()
            far(q, side).wait_send()
            cross(q, side).wait_send()
        swap(q).wait_send()
        return carry

    lax.fori_loop(0, NZ, drain, 0)
    own = f_ref[g // 8, (g // 4) % 2, (g // 2) % 2, g % 2]
    pre = jnp.dot(own, ws_ref[...], precision=HIGH, preferred_element_type=F32) + b_ref[...]
    end_grp(send_sum)
    whole = u_ref[g]
    for k in range(1, GRP):
        whole = whole + r1[k]
    at = g * share + lax.broadcasted_iota(jnp.int32, (share, tile), 0)
    lane = lax.broadcasted_iota(jnp.int32, (share, tile), 1)
    degree = jnp.zeros((share, tile), F32)
    for t in range(tblocks):
        row = jnp.broadcast_to(whole[share + t : share + t + 1, :tile], (share, tile))
        degree = jnp.where(at == t * tile + lane, row, degree)
    degree = jnp.sum(degree, axis=1, keepdims=True)
    neigh = whole[:share] / jnp.sqrt(1.0 + degree)
    pre = pre + jnp.dot(neigh, wn_ref[...], precision=HIGH, preferred_element_type=F32)
    sig = jax.nn.sigmoid(pre)
    layer_ref[...] = pre * sig
    dpre = cot_ref[...] * sig * (1.0 + pre * (1.0 - sig))
    dims = (((0,), (0,)), ((), ()))
    halves = (own, neigh)
    for n in range(2):
        grad = lax.dot_general(halves[n], dpre, dims, precision=HIGH, preferred_element_type=F32)
        for k in range(8):
            for t in range(8):
                low, col = k * 32 + (t // 2) * 8, (t % 2) * 128
                part[n * 8 + k, t] = grad[low : low + 8, col : col + 128]
    sums = jnp.sum(dpre, axis=0, keepdims=True)
    first = jnp.broadcast_to(sums[:, :128], (8, 128))
    second = jnp.broadcast_to(sums[:, 128:], (8, 128))
    bias_tile = jnp.where(line == 0, first, jnp.where(line == 1, second, 0.0))
    for k in range(GRP):
        part[k, 8] = bias_tile

    def send_part(k):
        peer = (g + k) % GRP
        return remote(part.at[peer], r2.at[k], s2.at[k], q2.at[k], (peer, m))

    over_grp(send_part)
    end_grp(send_part)
    acc = part[g]
    for k in range(1, GRP):
        acc = acc + r2[k]
    mine[...] = acc

    def send_tile(k):
        to = owner_of(k)
        away = (to - m + MEM) % MEM
        return remote(mine.at[k], r3.at[away], s3.at[k], q3.at[away], (g, to))

    def start_tile(k, carry):
        @pl.when(owner_of(k) != m)
        def _():
            send_tile(k).start()

        return carry

    lax.fori_loop(0, TILES, start_tile, 0)
    zz = m % NZ
    mine_k = (zz // 3) * 2 + m // NZ
    is_owner = (zz % 3 == 0) & (mine_k < TILES)

    def hand_out(k):
        return remote(total, fin.at[mine_k], s4.at[k], q4.at[mine_k], (g, (m + k) % MEM))

    @pl.when(is_owner)
    def _():
        def arrive(k, carry):
            remote(mine.at[0], r3.at[k], s3.at[0], q3.at[k], (g, (m + k) % MEM)).wait_recv()
            return carry

        lax.fori_loop(1, MEM, arrive, 0)
        acc = mine[mine_k]
        for k in range(1, MEM):
            acc = acc + r3[k]
        total[...] = acc
        fin[mine_k] = acc

        def give(t, carry):
            d = NZ // 2 - t
            hand_out(d).start()
            hand_out(NZ + d).start()

            @pl.when(t > 0)
            def _():
                hand_out(NZ - d).start()
                hand_out(2 * NZ - d).start()

            return carry

        lax.fori_loop(0, NZ // 2, give, 0)
        hand_out(NZ).start()

    def take_tile(k, carry):
        @pl.when(owner_of(k) != m)
        def _():
            remote(total, fin.at[k], s4.at[0], q4.at[k], (g, owner_of(k))).wait_recv()
            send_tile(k).wait_send()

        return carry

    lax.fori_loop(0, TILES, take_tile, 0)

    def send_fin(k):
        peer = (g + k) % GRP
        return remote(fin.at[pl.ds(0, 8)], grad_ref.at[g], s5.at[k], q5.at[k], (peer, m))

    def recv_fin(k):
        peer = (g + GRP - k) % GRP
        return remote(fin.at[pl.ds(0, 8)], grad_ref.at[peer], s5.at[k], q5.at[k], (peer, m))

    over_grp(send_fin)
    grad_ref[g] = fin[0:8]
    bias_ref[...] = fin[8]

    def finish(k, carry):
        send_fin(k).wait_send()
        recv_fin(k).wait_recv()
        return carry

    lax.fori_loop(1, GRP, finish, 0)

    @pl.when(is_owner)
    def _():
        def done(k, carry):
            hand_out(k).wait_send()
            return carry

        lax.fori_loop(1, MEM, done, 0)


def pack_kernel(layer_ref, tiles_ref, bias_ref, layer_out, self_out, neigh_out, bias_out):
    layer_out[...] = layer_ref[...]
    for n, out in enumerate((self_out, neigh_out)):
        for k in range(8):
            for t in range(8):
                low, col = k * 32 + (t // 2) * 8, (t % 2) * 128
                out[low : low + 8, col : col + 128] = tiles_ref[n * 8 + k, t]
    bias_out[:, :128] = bias_ref[0:1]
    bias_out[:, 128:] = bias_ref[1:2]


def on_device(features, patterns, src_tile, dst_tile, tile_count, cotangent, w_self, w_neigh, bias):
    block, width = features.shape
    share = cotangent.shape[0]
    members, slots, tile, _ = patterns.shape[2:]
    tblocks = block // tile
    dma = pltpu.SemaphoreType.DMA
    vmem = pl.BlockSpec(memory_space=pltpu.VMEM)
    smem = pl.BlockSpec(memory_space=pltpu.SMEM)
    layer, tiles, bias_tile = pl.pallas_call(
        kernel,
        out_shape=(
            jax.ShapeDtypeStruct((share, width), F32),
            jax.ShapeDtypeStruct((GRP, 8, 8, 128), F32),
            jax.ShapeDtypeStruct((8, 128), F32),
        ),
        in_specs=[smem] * 3 + [vmem] * 6,
        out_specs=(vmem, vmem, vmem),
        scratch_shapes=[
            pltpu.VMEM((NZ, 2, 2, 2, NY, share, width), F32),
            pltpu.VMEM((2, tblocks, 2 * tile, width), jnp.bfloat16),
            pltpu.VMEM((block, width), F32),
            pltpu.VMEM((block, tile), F32),
            pltpu.VMEM((GRP, share + 8, width), F32),
            pltpu.VMEM((GRP, share + 8, width), F32),
            pltpu.VMEM((GRP, TILES, 8, 128), F32),
            pltpu.VMEM((GRP, TILES, 8, 128), F32),
            pltpu.VMEM((TILES, 8, 128), F32),
            pltpu.VMEM((MEM, 8, 128), F32),
            pltpu.VMEM((8, 128), F32),
            pltpu.VMEM((TILES, 8, 128), F32),
            dma((NZ,)), dma((NZ,)),
            dma((NZ, 2)), dma((NZ, 2)),
            dma((NZ, 2)), dma((NZ, 2)),
            dma((NZ, 2)), dma((NZ, 2)),
            dma((NZ,)), dma((NZ,)),
            dma(()),
            dma((GRP,)), dma((GRP,)),
            dma((GRP,)), dma((GRP,)),
            dma((TILES,)), dma((MEM,)),
            dma((MEM,)), dma((TILES,)),
            dma((GRP,)), dma((GRP,)),
        ],
        compiler_params=pltpu.CompilerParams(collective_id=0, has_side_effects=True),
    )(
        src_tile[0, 0].T,
        dst_tile[0, 0].T,
        tile_count,
        features.reshape(2, 2, 2, 2, share, width),
        patterns.reshape(2, NZ, slots, tile, tile),
        cotangent,
        w_self,
        w_neigh,
        bias.reshape(1, width),
    )
    layer, grad_self, grad_neigh, grad_bias = pl.pallas_call(
        pack_kernel,
        out_shape=(
            jax.ShapeDtypeStruct((share, width), F32),
            jax.ShapeDtypeStruct((width, width), F32),
            jax.ShapeDtypeStruct((width, width), F32),
            jax.ShapeDtypeStruct((1, width), F32),
        ),
        in_specs=[vmem] * 3,
        out_specs=(vmem,) * 4,
    )(layer, tiles, bias_tile)
    return layer, grad_self, grad_neigh, grad_bias.reshape(width)


def solution(mesh):
    placed = (
        P("mem", None),
        P("grp", "mem", None, None, None, None),
        P("grp", "mem", None, None),
        P("grp", "mem", None, None),
        P("grp", "mem"),
        P(("mem", "grp"), None),
        P(),
        P(),
        P(),
    )
    return jax.shard_map(
        on_device,
        mesh=mesh,
        in_specs=placed,
        out_specs=(P(("mem", "grp"), None), P(), P(), P()),
        check_vma=False,
    )
```
